32 devices in a mesh: dp: 4 (over x, core), row: 4 (over z), col: 2 (over y).
Axes of the slice: x: 2, y: 2, z: 4, core: 2. Of those that a mesh axis runs over, the one named last changes fastest.
Arguments:
- features: bfloat16 [16, 768, 512], P(('dp', 'col'), 'row'), may hold values from -6 to 6
- cotangent: bfloat16 [16, 768, 512], P(('dp', 'col'), 'row'), may hold values from -6 to 6
- query_weight: bfloat16 [768, 768], P('row', 'col'), may hold values from -0.21875 to 0.21875
- key_weight: bfloat16 [768, 768], P('row', 'col'), may hold values from -0.21875 to 0.21875
- value_weight: bfloat16 [768, 768], P('row', 'col'), may hold values from -0.21875 to 0.21875
- query_bias: float32 [768], P('col'), may hold values from -3 to 3
- value_bias: float32 [768], P('col'), may hold values from -1.2 to 1.2
- out_weight: bfloat16 [768, 768], P('row', 'col'), may hold values from -1.25 to 1.25
- out_bias: float32 [768], replicated, may hold values from -1.8 to 1.8
- fc1_weight: bfloat16 [768, 3072], P('row', 'col'), may hold values from -0.21875 to 0.21875
- fc1_bias: float32 [3072], P('col'), may hold values from -1.8 to 1.8
- fc2_weight: bfloat16 [768, 3072], P('row', 'col'), may hold values from -0.109375 to 0.109375
- fc2_bias: float32 [768], replicated, may hold values from -1.8 to 1.8
- norm1_gain: float32 [768], replicated, may hold values from 0.5 to 1.5
- norm1_shift: float32 [768], replicated, may hold values from -1.8 to 1.8
- norm2_gain: float32 [768], replicated, may hold values from 0.5 to 1.5
- norm2_shift: float32 [768], replicated, may hold values from -1.8 to 1.8
Outputs:
- output: bfloat16 [16, 768, 512], P(('dp', 'col'), 'row')
- features_grad: float32 [16, 768, 512], P(('dp', 'col'), 'row')
- query_weight_grad: float32 [768, 768], P('row', 'col')
- key_weight_grad: float32 [768, 768], P('row', 'col')
- value_weight_grad: float32 [768, 768], P('row', 'col')
- query_bias_grad: float32 [768], P('col')
- value_bias_grad: float32 [768], P('col')
- out_weight_grad: float32 [768, 768], P('row', 'col')
- out_bias_grad: float32 [768], P('row')
- fc1_weight_grad: float32 [768, 3072], P('row', 'col')
- fc1_bias_grad: float32 [3072], P('col')
- fc2_weight_grad: float32 [768, 3072], P('row', 'col')
- fc2_bias_grad: float32 [768], P('row')
- norm1_gain_grad: float32 [768], P('row')
- norm1_shift_grad: float32 [768], P('row')
- norm2_gain_grad: float32 [768], P('row')
- norm2_shift_grad: float32 [768], P('row')
The draws below stay inside these ranges and needn't reach their ends.
All inputs are finite; a program needn't handle non-finite values.
Results may differ from the reference program's by a relative error of at most 0.017.
Values may be sent and summed in bfloat16 or wider, within the bound.
No kernel may reach another device: no remote copies, remote signals or barrier semaphores. Data moves between devices by JAX's collectives and lax.ppermute only.
A program may use at most 192 MiB of HBM per device.

```python
import math
import jax
import jax.numpy as jnp
from jax import lax

D = 768
FF = 3072
LEN = 512
QBLOCK = 512
HEAD_DIM = 64
CLIPS = 16


def level_of(stream_key, dims, split, least, top_value):
    gain = 1.0
    for position, shards_of in split:
        draws = jax.random.uniform(jax.random.fold_in(jax.random.fold_in(stream_key, 6), position), (shards_of,), jnp.float32, least / len(split), top_value / len(split))
        gain = gain * jnp.repeat(jnp.exp(draws), dims[position] // shards_of).reshape((-1,) + (1,) * (len(dims) - 1 - position))
    return gain


def bell_draw(key, extent, deviation, most, shards=(), dtype=jnp.bfloat16):
    values = jax.random.normal(key, extent, jnp.float32) * deviation
    if len(shards) > 0:
        values = level_of(key, extent, shards, -0.22, 0.18) * values
    return jnp.clip(values, min=-most, max=most).astype(dtype)


def setup_inputs(seed: int = 0) -> dict:
    arg_keys = jax.random.split(jax.random.key(seed), 18)
    features = bell_draw(arg_keys[0], (CLIPS, D, LEN), 1.0, 6.0, ((0, 8), (1, 4)))
    cotangent = bell_draw(arg_keys[1], (CLIPS, D, LEN), 1.0, 6.0, ((0, 8), (1, 4)))
    query_weight = bell_draw(arg_keys[2], (D, D), D ** -0.5, 0.21875, ((0, 4), (1, 2)))
    key_weight = bell_draw(arg_keys[3], (D, D), D ** -0.5, 0.21875, ((0, 4), (1, 2)))
    value_weight = bell_draw(arg_keys[4], (D, D), D ** -0.5, 0.21875, ((0, 4), (1, 2)))
    query_bias = bell_draw(arg_keys[5], (D,), 0.5, 3.0, ((0, 2),), jnp.float32)
    value_bias = bell_draw(arg_keys[6], (D,), 0.2, 1.2, ((0, 2),), jnp.float32)
    out_weight = bell_draw(arg_keys[7], (D, D), (D // 32) ** -0.5, 1.25, ((0, 4), (1, 2)))
    out_bias = bell_draw(arg_keys[8], (D,), 0.3, 1.8, (), jnp.float32)
    fc1_weight = bell_draw(arg_keys[9], (D, FF), D ** -0.5, 0.21875, ((0, 4), (1, 2)))
    fc1_bias = bell_draw(arg_keys[10], (FF,), 0.3, 1.8, ((0, 2),), jnp.float32)
    fc2_weight = bell_draw(arg_keys[11], (D, FF), FF ** -0.5, 0.109375, ((0, 4), (1, 2)))
    fc2_bias = bell_draw(arg_keys[12], (D,), 0.3, 1.8, (), jnp.float32)
    norm1_gain = jnp.clip(1.0 + 0.1 * jax.random.normal(arg_keys[13], (D,), jnp.float32), 0.5, 1.5)
    norm1_shift = bell_draw(arg_keys[14], (D,), 0.3, 1.8, (), jnp.float32)
    norm2_gain = jnp.clip(1.0 + 0.1 * jax.random.normal(arg_keys[15], (D,), jnp.float32), 0.5, 1.5)
    norm2_shift = bell_draw(arg_keys[16], (D,), 0.3, 1.8, (), jnp.float32)
    return {"features": features, "cotangent": cotangent, "query_weight": query_weight, "key_weight": key_weight, "value_weight": value_weight, "query_bias": query_bias, "value_bias": value_bias, "out_weight": out_weight, "out_bias": out_bias, "fc1_weight": fc1_weight, "fc1_bias": fc1_bias, "fc2_weight": fc2_weight, "fc2_bias": fc2_bias, "norm1_gain": norm1_gain, "norm1_shift": norm1_shift, "norm2_gain": norm2_gain, "norm2_shift": norm2_shift}


@jax.custom_vjp
def low(v):
    return lax.optimization_barrier(v.astype(jnp.bfloat16)).astype(jnp.float32)

@jax.custom_vjp
def low_back(v):
    return v

def low_keep(v):
    return (low(v), None)

def low_pass(kept, grad):
    return (grad,)

def back_keep(v):
    return (v, None)

def back_low(kept, grad):
    return (low(grad),)
low.defvjp(low_keep, low_pass)
low_back.defvjp(back_keep, back_low)
eps_norm = 1e-05

def matmul(left, right):
    return jnp.dot(left, right, precision=lax.Precision.HIGHEST)

def layer_norm(stream, norm_gain, norm_shift):
    row_mean = lax.optimization_barrier(jnp.mean(stream, axis=-1, keepdims=True))
    centred = stream - row_mean
    spread = lax.optimization_barrier(jnp.mean(centred * centred, axis=-1, keepdims=True))
    return centred * lax.rsqrt(spread + eps_norm) * norm_gain + norm_shift

def attention_block(block_q, keys, values):
    factor = 1.0 / math.sqrt(HEAD_DIM)
    logits = low_back(jnp.einsum('qhd,khd->hqk', block_q, keys, precision=lax.Precision.HIGHEST) * factor)
    row_peak = lax.optimization_barrier(jnp.max(logits, axis=-1, keepdims=True))
    weights = jnp.exp(logits - row_peak)
    probs = weights / lax.optimization_barrier(jnp.sum(weights, axis=-1, keepdims=True))
    return jnp.einsum('hqk,khd->qhd', low(probs), values, precision=lax.Precision.HIGHEST)

def one_clip(params, single_clip):
    query_weight, key_weight, value_weight, query_bias, value_bias, out_weight, out_bias, fc1_weight, fc1_bias, fc2_weight, fc2_bias, norm1_gain, norm1_shift, norm2_gain, norm2_shift = params
    frames = single_clip.T
    normed_one = low(layer_norm(frames, norm1_gain, norm1_shift))
    queries = low(low_back(matmul(normed_one, query_weight) + query_bias))
    keys = low(low_back(matmul(normed_one, key_weight)))
    values = low(low_back(matmul(normed_one, value_weight) + value_bias))
    heads = D // HEAD_DIM
    shaped_q = queries.reshape(LEN // QBLOCK, QBLOCK, heads, HEAD_DIM)
    shaped_k = keys.reshape(LEN, heads, HEAD_DIM)
    shaped_v = values.reshape(LEN, heads, HEAD_DIM)
    mixed = lax.map(jax.checkpoint(lambda block_q: attention_block(block_q, shaped_k, shaped_v)), shaped_q)
    mixed = low(low_back(mixed.reshape(LEN, D)))
    middle = frames + low_back(matmul(mixed, out_weight.T) + out_bias)
    normed_two = low(layer_norm(middle, norm2_gain, norm2_shift))
    hidden_pre = low_back(matmul(normed_two, fc1_weight) + fc1_bias)
    activ = low(jax.nn.gelu(hidden_pre, approximate=False))
    result = middle + low_back(matmul(activ, fc2_weight.T) + fc2_bias)
    return result.T

def forward(params, stream):
    return lax.map(jax.checkpoint(lambda single_clip: one_clip(params, single_clip)), stream)

def reference(features, cotangent, query_weight, key_weight, value_weight, query_bias, value_bias, out_weight, out_bias, fc1_weight, fc1_bias, fc2_weight, fc2_bias, norm1_gain, norm1_shift, norm2_gain, norm2_shift):
    params = (query_weight.astype(jnp.float32), key_weight.astype(jnp.float32), value_weight.astype(jnp.float32), query_bias.astype(jnp.float32), value_bias.astype(jnp.float32), out_weight.astype(jnp.float32), out_bias.astype(jnp.float32), fc1_weight.astype(jnp.float32), fc1_bias.astype(jnp.float32), fc2_weight.astype(jnp.float32), fc2_bias.astype(jnp.float32), norm1_gain.astype(jnp.float32), norm1_shift.astype(jnp.float32), norm2_gain.astype(jnp.float32), norm2_shift.astype(jnp.float32))
    stream = features.astype(jnp.float32)
    result, pullback = jax.vjp(forward, params, stream)
    param_grads, features_grad = pullback(cotangent.astype(jnp.float32))
    return (result.astype(jnp.bfloat16), features_grad, param_grads[0], param_grads[1], param_grads[2], param_grads[3], param_grads[4], param_grads[5], param_grads[6], param_grads[7], param_grads[8], param_grads[9], param_grads[10], param_grads[11], param_grads[12], param_grads[13], param_grads[14])
```

```python
import math

import jax
import jax.numpy as jnp
import numpy as np
from jax import lax
from jax.sharding import Mesh
from jax.sharding import PartitionSpec as P

HEAD_DIM = 64
EPS = 1e-05
BF = jnp.bfloat16
F32 = jnp.float32


def dot(left, right, dims):
    return lax.dot_general(left, right, (dims, ((), ())), preferred_element_type=F32)


def add_low(left, right):
    return (left.astype(F32) + right.astype(F32)).astype(BF)


class Links:
    def __init__(self, count_x, count_row):
        self.count_x = count_x
        self.count_row = count_row
        self.x = lax.axis_index("x")
        self.core = lax.axis_index("core")
        self.row = lax.axis_index("row")
        self.col = lax.axis_index("col")
        self.primary = self.core == self.col

    def swap(self, value, axis, mask=1):
        size = lax.axis_size(axis)
        return lax.ppermute(value, axis, [(i, i ^ mask) for i in range(size)])

    def row_swap_primary(self, value, mask):
        rows = self.count_row

        def place(core, row):
            return (core * rows + row) * 2 + core

        pairs = [(place(k, r), place(k, r ^ mask)) for k in range(2) for r in range(rows)]
        return lax.ppermute(value, ("core", "row", "col"), pairs)

    def x_swap_primary(self, value, mask):
        def place(x, core):
            return (x * 2 + core) * 2 + core

        pairs = [(place(x, k), place(x ^ mask, k)) for k in range(2) for x in range(self.count_x)]
        return lax.ppermute(value, ("x", "core", "col"), pairs)

    def primary_to_secondary(self, value):
        return lax.ppermute(value, ("core", "col"), [(0, 1), (3, 2)])

    def secondary_to_primary(self, value):
        return lax.ppermute(value, ("core", "col"), [(1, 0), (2, 3)])

    def primary_to_partner(self, value):
        return lax.ppermute(value, ("core", "col"), [(0, 2), (3, 1)])

    def row_gather(self, piece):
        held = piece[None]
        mask = 1
        while mask < self.count_row:
            held = jnp.concatenate([held, self.row_swap_primary(held, mask)], axis=0)
            mask *= 2
        return held

    def x_gather(self, held, swap):
        mask = 1
        while mask < self.count_x:
            other = swap(held, mask)
            first = (self.x & mask) == 0
            held = jnp.concatenate(
                [jnp.where(first, held, other), jnp.where(first, other, held)], axis=1
            )
            mask *= 2
        return held

    def gather(self, block, splits):
        height = block.shape[0] // self.count_x
        piece = lax.dynamic_slice_in_dim(block, self.x * height, height, 0)
        held = self.row_gather(piece)
        results = []
        for start, stop, order in splits:
            part = held[:, :, start:stop]
            if order == "yx":
                part = jnp.where(self.primary, part, self.primary_to_secondary(part))
                part = self.x_gather(part, lambda v, m: self.swap(v, "x", m))
            else:
                part = self.x_gather(part, self.x_swap_primary)
                part = jnp.where(self.primary, part, self.primary_to_secondary(part))
            results.append(part.reshape(-1, stop - start))
        return results

    def x_scatter(self, grad, swap):
        mask = self.count_x // 2
        while mask >= 1:
            half = grad.shape[1] // 2
            first = (self.x & mask) == 0
            low, high = grad[:, :half], grad[:, half:]
            keep = jnp.where(first, low, high)
            grad = add_low(keep, swap(jnp.where(first, high, low), mask))
            mask //= 2
        return grad

    def reduce(self, grad, order):
        grad = grad.astype(BF).reshape(self.count_row, -1, grad.shape[1])
        if order == "xy":
            grad = self.x_scatter(grad, lambda v, m: self.swap(v, "x", m))
            grad = add_low(grad, self.secondary_to_primary(grad))
        else:
            grad = add_low(grad, self.secondary_to_primary(grad))
            grad = self.x_scatter(grad, self.x_swap_primary)
        mask = self.count_row // 2
        while mask >= 1:
            grad = add_low(grad[:mask], self.row_swap_primary(grad[mask:], mask))
            mask //= 2
        block = self.x_gather(grad, self.x_swap_primary)[0]
        return jnp.where(self.primary, block, self.primary_to_partner(block)).astype(F32)

    def by_core(self, mine, other, axis):
        first = self.core == 0
        return jnp.concatenate(
            [jnp.where(first, mine, other), jnp.where(first, other, mine)], axis=axis
        )

    def frames_half(self, value, which):
        half = value.shape[-1] // 2
        return lax.dynamic_slice_in_dim(value, which * half, half, value.ndim - 1)

    def clips_in(self, local):
        kinds, clips, width, length = local.shape
        mine = self.frames_half(local, self.core)
        other = self.swap(self.frames_half(local, 1 - self.core), "core")
        pieces = self.by_core(mine, other, 1)
        held = jnp.stack(
            [
                lax.dynamic_index_in_dim(pieces, self.row ^ j, 1, keepdims=False)
                for j in range(self.count_row)
            ]
        )
        held = held[None]
        mask = 1
        while mask < self.count_row:
            moved = self.swap(held[:, 1::2], "row", mask)
            held = jnp.concatenate([held[:, 0::2], moved], axis=0)
            mask *= 2
        held = held[:, 0]
        held = jnp.moveaxis(held, 0, 1).reshape(kinds, self.count_row * width, length // 2)
        return self.by_core(held, self.swap(held, "core"), 2)

    def clips_out(self, half, clips):
        width = half.shape[0] // self.count_row
        held = half.reshape(self.count_row, 1, width, half.shape[1])
        mask = 1
        while mask < self.count_row:
            moved = self.swap(held[1::2], "row", mask)
            held = jnp.concatenate([held[0::2], moved], axis=1)
            mask *= 2
        held = held[0]
        order = [0]
        mask = 1
        while mask < self.count_row:
            order = order + [o + mask for o in order]
            mask *= 2
        place = [order.index(j) for j in range(self.count_row)]
        held = held[np.array(place)] if place != list(range(self.count_row)) else held

        def clip(index):
            return lax.dynamic_index_in_dim(held, self.row ^ index, 0, keepdims=False)

        mine = jnp.stack([clip(self.core * clips + i) for i in range(clips)])
        give = jnp.stack([clip((1 - self.core) * clips + i) for i in range(clips)])
        return self.by_core(mine, self.swap(give, "core"), 2)


def unit_of(stream):
    mean = jnp.mean(stream, axis=0, keepdims=True)
    centred = stream - mean
    inverse = lax.rsqrt(jnp.mean(centred * centred, axis=0, keepdims=True) + EPS)
    return centred * inverse, inverse


def norm_back(grad, unit, inverse, gain):
    scaled = grad * gain
    first = jnp.mean(scaled, axis=0, keepdims=True)
    second = jnp.mean(scaled * unit, axis=0, keepdims=True)
    return inverse * (scaled - first - unit * second)


def gelu_exact(operand):
    return jax.nn.gelu(operand, approximate=False)


def attend(queries, keys, values):
    logits = jnp.einsum("heq,hek->hqk", queries, keys, preferred_element_type=F32) * (
        1.0 / math.sqrt(HEAD_DIM)
    )
    peak = jnp.max(logits, axis=-1, keepdims=True)
    weights = jnp.exp(logits - peak)
    total = jnp.sum(weights, axis=-1, keepdims=True)
    probs = weights / total
    mixed = jnp.einsum("hqk,hek->heq", probs.astype(BF), values, preferred_element_type=F32)
    return mixed.astype(BF), peak + jnp.log(total)


def attend_back(queries, keys, values, norms, grad_mixed):
    factor = 1.0 / math.sqrt(HEAD_DIM)
    logits = jnp.einsum("heq,hek->hqk", queries, keys, preferred_element_type=F32) * factor
    probs = jnp.exp(logits - norms)
    grad_v = jnp.einsum("hqk,heq->hek", probs.astype(BF), grad_mixed, preferred_element_type=F32)
    grad_p = jnp.einsum("heq,hek->hqk", grad_mixed, values, preferred_element_type=F32)
    inner = jnp.sum(probs * grad_p, axis=-1, keepdims=True)
    grad_s = (probs * (grad_p - inner)).astype(BF)
    grad_q = jnp.einsum("hqk,hek->heq", grad_s, keys, preferred_element_type=F32) * factor
    grad_k = jnp.einsum("hqk,heq->hek", grad_s, queries, preferred_element_type=F32) * factor
    return grad_q, grad_k, grad_v


def on_device(
    features,
    cotangent,
    query_weight,
    key_weight,
    value_weight,
    query_bias,
    value_bias,
    out_weight,
    out_bias,
    fc1_weight,
    fc1_bias,
    fc2_weight,
    fc2_bias,
    norm1_gain,
    norm1_shift,
    norm2_gain,
    norm2_shift,
):
    clips, width, length = features.shape
    count_row = lax.axis_size("row")
    links = Links(lax.axis_size("x"), count_row)
    assert 2 * clips == count_row
    split = query_weight.shape[1]
    hidden = fc1_weight.shape[1]
    heads = split // HEAD_DIM
    row = links.row

    def ordered(vector):
        return jnp.concatenate(
            [
                lax.dynamic_slice_in_dim(vector, (row ^ j) * width, width, 0)
                for j in range(count_row)
            ]
        )[:, None]

    biases = jnp.concatenate([query_bias, value_bias, fc1_bias])
    biases = jnp.where(links.primary, biases, links.swap(biases, "col"))
    bias_q, bias_v, bias_1 = biases[:split], biases[split : 2 * split], biases[2 * split :]
    qkv_bias = jnp.concatenate([bias_q, jnp.zeros_like(bias_q), bias_v])[:, None]

    attn_block = jnp.concatenate([query_weight, key_weight, value_weight, out_weight], axis=1)
    w_qk, w_vo = links.gather(attn_block, [(0, 2 * split, "yx"), (2 * split, 4 * split, "xy")])
    w_qkv = jnp.concatenate([w_qk, w_vo[:, :split]], axis=1)
    w_o = w_vo[:, split:]
    both = links.clips_in(jnp.stack([features, cotangent]))
    half_hidden = hidden // 2
    pieces = [(0, half_hidden, "yx"), (half_hidden, hidden, "xy")]
    w_1 = jnp.concatenate(links.gather(fc1_weight, pieces), axis=1)
    w_2 = jnp.concatenate(links.gather(fc2_weight, pieces), axis=1)

    stream = both[0].astype(F32)
    grad_out = both[1]
    upstream = grad_out.astype(F32)
    gain_1, gain_2 = ordered(norm1_gain), ordered(norm2_gain)

    unit_1, inverse_1 = unit_of(stream)
    normed_1 = (unit_1 * gain_1 + ordered(norm1_shift)).astype(BF)
    qkv = (dot(w_qkv, normed_1, ((0,), (0,))) + qkv_bias).astype(BF)
    queries, keys, values = qkv.reshape(3, heads, HEAD_DIM, length)
    mixed_heads, log_norms = attend(queries, keys, values)
    mixed = mixed_heads.reshape(split, length)
    attn_part = dot(w_o, mixed, ((1,), (0,)))
    attn_out = attn_part + links.swap(attn_part.astype(BF), "core").astype(F32)
    middle = stream + (attn_out + ordered(out_bias))
    unit_2, inverse_2 = unit_of(middle)
    normed_2 = (unit_2 * gain_2 + ordered(norm2_shift)).astype(BF)
    hidden_pre = dot(w_1, normed_2, ((0,), (0,))) + bias_1[:, None]
    activ, gelu_pullback = jax.vjp(gelu_exact, hidden_pre)
    activ = activ.astype(BF)

    fc2_part = dot(grad_out, activ, ((1,), (1,)))
    fc2_grad = links.reduce(fc2_part, "yx")

    (grad_hidden,) = gelu_pullback(dot(w_2, grad_out, ((0,), (0,))))
    grad_hidden = grad_hidden.astype(BF)
    fc1_part = dot(normed_2, grad_hidden, ((1,), (1,)))
    fc1_grad = links.reduce(fc1_part, "yx")

    ffn_part = dot(w_2, activ, ((1,), (0,)))

    def core_sum(part):
        other = links.swap(links.frames_half(part, 1 - links.core).astype(BF), "core")
        return links.frames_half(part, links.core) + other.astype(F32)

    out_half = links.frames_half(middle, links.core) + (core_sum(ffn_part) + ordered(fc2_bias))
    output = links.clips_out(out_half.astype(BF), clips)

    normed_2_part = dot(w_1, grad_hidden, ((1,), (0,)))
    grad_normed_2 = normed_2_part + links.swap(normed_2_part.astype(BF), "core").astype(F32)
    middle_grad = upstream + norm_back(grad_normed_2, unit_2, inverse_2, gain_2)
    grad_branch = middle_grad.astype(BF)
    out_part = dot(grad_branch, mixed, ((1,), (1,)))
    grad_mixed = dot(w_o, grad_branch, ((0,), (0,))).astype(BF)
    grads = attend_back(
        queries, keys, values, log_norms, grad_mixed.reshape(heads, HEAD_DIM, length)
    )
    grad_qkv = jnp.concatenate([g.reshape(split, length) for g in grads], axis=0).astype(BF)
    qkv_part = dot(normed_1, grad_qkv, ((1,), (1,)))
    qk_grad = links.reduce(qkv_part[:, : 2 * split], "xy")
    vo_grad = links.reduce(jnp.concatenate([qkv_part[:, 2 * split :], out_part], axis=1), "yx")
    normed_1_part = dot(w_qkv, grad_qkv, ((1,), (0,)))
    grad_normed_1 = core_sum(normed_1_part)
    unit_1_half = links.frames_half(unit_1, links.core)
    features_half = links.frames_half(middle_grad, links.core) + norm_back(
        grad_normed_1, unit_1_half, links.frames_half(inverse_1, links.core), gain_1
    )
    features_grad = links.clips_out(features_half.astype(BF), clips).astype(F32)

    def mine(value):
        return jnp.sum(links.frames_half(value, links.core).astype(F32), axis=1)

    grad_normed_2_half = links.frames_half(grad_normed_2, links.core)
    by_width = jnp.stack(
        [
            jnp.sum(grad_normed_1 * unit_1_half, axis=1),
            jnp.sum(grad_normed_1, axis=1),
            jnp.sum(grad_normed_2_half * links.frames_half(unit_2, links.core), axis=1),
            jnp.sum(grad_normed_2_half, axis=1),
            mine(grad_branch),
            mine(grad_out),
        ]
    ).reshape(6, count_row, width)
    by_width = jnp.stack(
        [lax.dynamic_index_in_dim(by_width, row ^ j, 1, keepdims=False) for j in range(count_row)],
        axis=1,
    )
    sums_qkv = jnp.sum(grad_qkv.astype(F32), axis=1)
    by_column = jnp.concatenate(
        [sums_qkv[:split], sums_qkv[2 * split :], jnp.sum(grad_hidden.astype(F32), axis=1)]
    )
    zeros = jnp.zeros_like(by_column)
    first = links.core == 0
    packed = jnp.concatenate(
        [by_width.reshape(-1), jnp.where(first, by_column, zeros), jnp.where(first, zeros, by_column)]
    )
    packed = lax.psum(packed, ("x", "core", "row", "col"))
    size = 6 * count_row * width
    by_width = lax.dynamic_index_in_dim(
        packed[:size].reshape(6, count_row, width), row, 1, keepdims=False
    )
    by_column = lax.dynamic_index_in_dim(packed[size:].reshape(2, -1), links.col, 0, keepdims=False)
    return (
        output,
        features_grad,
        qk_grad[:, :split],
        qk_grad[:, split:],
        vo_grad[:, :split],
        by_column[:split],
        by_column[split : 2 * split],
        vo_grad[:, split:],
        by_width[4],
        fc1_grad,
        by_column[2 * split :],
        fc2_grad,
        by_width[5],
        by_width[0],
        by_width[1],
        by_width[2],
        by_width[3],
    )


def solution(mesh):
    count_dp, count_row, count_col = mesh.devices.shape
    fine = Mesh(
        mesh.devices.reshape(count_dp // 2, 2, count_row, count_col), ("x", "core", "row", "col")
    )
    clip = P(("x", "core", "col"), "row", None)
    block, column, row, whole = P("row", "col"), P("col"), P("row"), P()
    return jax.shard_map(
        on_device,
        mesh=fine,
        in_specs=(
            clip,
            clip,
            block,
            block,
            block,
            column,
            column,
            block,
            whole,
            block,
            column,
            block,
            whole,
            whole,
            whole,
            whole,
            whole,
        ),
        out_specs=(
            clip,
            clip,
            block,
            block,
            block,
            column,
            column,
            block,
            row,
            block,
            column,
            block,
            row,
            row,
            row,
            row,
            row,
        ),
        check_vma=False,
    )
```

```python
import math

import jax
import jax.numpy as jnp
from jax import lax
from jax.sharding import Mesh
from jax.sharding import PartitionSpec as P

HEAD_DIM = 64
EPS = 1e-05
BF = jnp.bfloat16
F32 = jnp.float32


def dot(left, right, dims):
    return lax.dot_general(left, right, (dims, ((), ())), preferred_element_type=F32)


def add_low(left, right):
    return (left.astype(F32) + right.astype(F32)).astype(BF)


def doubled(count, low_first):
    masks = [1 << bit for bit in range(count.bit_length() - 1)]
    masks = masks if low_first else masks[::-1]
    order = [0]
    for mask in masks:
        order = order + [place ^ mask for place in order]
    return masks, order


def swap(value, axis, name, mask=1):
    with jax.named_scope(name):
        size = lax.axis_size(axis)
        return lax.ppermute(value, axis, [(i, i ^ mask) for i in range(size)])


def halves(value, which):
    half = value.shape[-1] // 2
    return lax.dynamic_slice_in_dim(value, which * half, half, value.ndim - 1)


def place(first, mine, other, axis):
    return jnp.concatenate([jnp.where(first, mine, other), jnp.where(first, other, mine)], axis=axis)


class Links:
    def __init__(self):
        self.count_x = lax.axis_size("x")
        self.count_row = lax.axis_size("row")
        self.x = lax.axis_index("x")
        self.core = lax.axis_index("core")
        self.row = lax.axis_index("row")
        self.col = lax.axis_index("col")
        self.down, self.order = doubled(self.count_row, False)
        self.up, _ = doubled(self.count_row, True)
        self.x_masks, self.x_order = doubled(self.count_x, True)

    def share(self, block, move=0):
        size = block.shape[-1] // (2 * self.count_x)
        return lax.dynamic_slice_in_dim(
            block, (self.core * self.count_x + (self.x ^ move)) * size, size, block.ndim - 1
        )

    def ordered(self, vector):
        parts = vector.reshape(self.count_row, -1)
        return jnp.concatenate(
            [lax.dynamic_index_in_dim(parts, self.row ^ j, 0, keepdims=False) for j in self.order]
        )[:, None]

    def row_gather(self, piece, name):
        held = piece[None]
        for mask in self.down:
            held = jnp.concatenate([held, swap(held, "row", f"{name}_z{mask}", mask)], axis=0)
        return held.reshape(-1, held.shape[-1])

    def gather_fixed(self, block, name):
        held = self.row_gather(self.share(block), name)
        for mask in self.x_masks:
            other = swap(held, "x", f"{name}_x{mask}", mask)
            held = place((self.x & mask) == 0, held, other, 1)
        return place(self.core == 0, held, swap(held, "core", f"{name}_c"), 1)

    def gather_halves(self, block, name):
        held = self.row_gather(self.share(block), name)
        for mask in self.x_masks:
            held = jnp.concatenate([held, swap(held, "x", f"{name}_x{mask}", mask)], axis=1)
        return held, swap(held, "core", f"{name}_c")

    def vector_halves(self, vector):
        parts = vector.reshape(2, self.count_x, -1)

        def half(core):
            mine = lax.dynamic_index_in_dim(parts, core, 0, keepdims=False)
            return jnp.concatenate(
                [
                    lax.dynamic_index_in_dim(mine, self.x ^ i, 0, keepdims=False)
                    for i in self.x_order
                ]
            )

        return half(self.core), half(1 - self.core)

    def vector_back(self, mine, other):
        def half(value):
            parts = value.reshape(self.count_x, -1)
            inverse = [self.x_order.index(i) for i in range(self.count_x)]
            parts = jnp.stack([parts[i] for i in inverse])
            return jnp.concatenate(
                [
                    lax.dynamic_index_in_dim(parts, self.x ^ i, 0, keepdims=False)
                    for i in range(self.count_x)
                ]
            )

        return place(self.core == 0, half(mine), half(other), 0)

    def row_scatter(self, grad, name):
        grad = grad.reshape(self.count_row, -1, grad.shape[1])
        for mask in self.up:
            half = grad.shape[0] // 2
            grad = add_low(grad[:half], swap(grad[half:], "row", f"{name}_z{mask}", mask))
        return grad[0]

    def spread(self, share, name):
        for mask in self.x_masks:
            other = swap(share, "x", f"{name}_g{mask}", mask)
            share = place((self.x & mask) == 0, share, other, share.ndim - 1)
        other = swap(share, "core", f"{name}_gc")
        return place(self.core == 0, share, other, share.ndim - 1).astype(F32)

    def reduce_x(self, grad, name):
        for mask in self.x_masks[::-1]:
            half = grad.shape[1] // 2
            grad = add_low(grad[:, :half], swap(grad[:, half:], "x", f"{name}_x{mask}", mask))
        return grad

    def reduce_x_fixed(self, grad, name):
        for mask in self.x_masks[::-1]:
            half = grad.shape[1] // 2
            first = (self.x & mask) == 0
            low, high = grad[:, :half], grad[:, half:]
            other = swap(jnp.where(first, high, low), "x", f"{name}_x{mask}", mask)
            grad = add_low(jnp.where(first, low, high), other)
        return grad

    def clip_in(self, local, name):
        first = self.col == 0
        mine = halves(local, self.col)
        pieces = place(first, mine, swap(halves(local, 1 - self.col), "col", f"{name}_y"), 0)
        held = jnp.stack(
            [
                lax.dynamic_index_in_dim(pieces, self.row ^ j, 0, keepdims=False)
                for j in range(self.count_row)
            ]
        )[None]
        for mask in self.down:
            half = held.shape[1] // 2
            moved = swap(held[:, half:], "row", f"{name}_z{mask}", mask)
            held = jnp.concatenate([held[:, :half], moved], axis=0)
        held = held.reshape(-1, held.shape[-1])
        return place(first, held, swap(held, "col", f"{name}_yg"), 1)

    def clip_out(self, half_frames, name):
        held = half_frames.reshape(self.count_row, 1, -1, half_frames.shape[-1])
        for mask in self.up:
            half = held.shape[0] // 2
            moved = swap(held[half:], "row", f"{name}_z{mask}", mask)
            held = jnp.concatenate([held[:half], moved], axis=1)
        held = held[0]
        clips = self.count_row // 2

        def of(col):
            return jnp.stack(
                [
                    lax.dynamic_index_in_dim(held, self.row ^ (col * clips + i), 0, keepdims=False)
                    for i in range(clips)
                ]
            )

        other = swap(of(1 - self.col), "col", f"{name}_y")
        return place(self.col == 0, of(self.col), other, 2)

    def col_sum(self, part, name):
        low = part.astype(BF)
        return low.astype(F32) + swap(low, "col", name).astype(F32)

    def col_scatter(self, part, name):
        other = swap(halves(part, 1 - self.col).astype(BF), "col", name)
        return halves(part, self.col) + other.astype(F32)


def unit_of(stream):
    mean = jnp.mean(stream, axis=0, keepdims=True)
    centred = stream - mean
    inverse = lax.rsqrt(jnp.mean(centred * centred, axis=0, keepdims=True) + EPS)
    return centred * inverse, inverse


def norm_back(grad, unit, inverse, gain):
    scaled = grad * gain
    first = jnp.mean(scaled, axis=0, keepdims=True)
    second = jnp.mean(scaled * unit, axis=0, keepdims=True)
    return inverse * (scaled - first - unit * second)


def gelu_parts(z):
    below = 0.5 + 0.5 * lax.erf(z * math.sqrt(0.5))
    return below, z * (jnp.exp(-0.5 * z * z) * (1.0 / math.sqrt(2.0 * math.pi)))


def attend(queries, keys, values):
    logits = jnp.einsum("heq,hek->hqk", queries, keys, preferred_element_type=F32) * (
        1.0 / math.sqrt(HEAD_DIM)
    )
    peak = jnp.max(logits, axis=-1, keepdims=True)
    weights = jnp.exp(logits - peak)
    total = jnp.sum(weights, axis=-1, keepdims=True)
    probs = weights / total
    mixed = jnp.einsum("hqk,hek->heq", probs.astype(BF), values, preferred_element_type=F32)
    return mixed.astype(BF), peak + jnp.log(total)


def attend_back(queries, keys, values, norms, grad_mixed):
    factor = 1.0 / math.sqrt(HEAD_DIM)
    logits = jnp.einsum("heq,hek->hqk", queries, keys, preferred_element_type=F32) * factor
    probs = jnp.exp(logits - norms)
    grad_v = jnp.einsum("hqk,heq->hek", probs.astype(BF), grad_mixed, preferred_element_type=F32)
    grad_p = jnp.einsum("heq,hek->hqk", grad_mixed, values, preferred_element_type=F32)
    inner = jnp.sum(probs * grad_p, axis=-1, keepdims=True)
    grad_s = (probs * (grad_p - inner)).astype(BF)
    grad_q = jnp.einsum("hqk,hek->heq", grad_s, keys, preferred_element_type=F32) * factor
    grad_k = jnp.einsum("hqk,heq->hek", grad_s, queries, preferred_element_type=F32) * factor
    return grad_q, grad_k, grad_v


def on_device(
    features,
    cotangent,
    query_weight,
    key_weight,
    value_weight,
    query_bias,
    value_bias,
    out_weight,
    out_bias,
    fc1_weight,
    fc1_bias,
    fc2_weight,
    fc2_bias,
    norm1_gain,
    norm1_shift,
    norm2_gain,
    norm2_shift,
):
    clips, width, length = features.shape
    links = Links()
    count_row, row, col, core = links.count_row, links.row, links.col, links.core
    assert 2 * clips == count_row
    split = query_weight.shape[1]
    heads = split // HEAD_DIM
    ordered = links.ordered

    attn_block = jnp.concatenate([query_weight, key_weight, value_weight, out_weight], axis=1)
    w_attn = links.gather_fixed(attn_block, "wa")
    stream = links.clip_in(features, "fi").astype(F32)
    w_1 = links.gather_halves(fc1_weight, "w1")
    w_2 = links.gather_halves(fc2_weight, "w2")
    grad_out = links.clip_in(cotangent, "ci")
    upstream = grad_out.astype(F32)
    w_qkv, w_o = w_attn[:, : 3 * split], w_attn[:, 3 * split :]
    gain_1, gain_2 = ordered(norm1_gain), ordered(norm2_gain)
    qkv_bias = jnp.concatenate([query_bias, jnp.zeros_like(query_bias), value_bias])[:, None]
    bias_1 = links.vector_halves(fc1_bias)

    unit_1, inverse_1 = unit_of(stream)
    normed_1 = (unit_1 * gain_1 + ordered(norm1_shift)).astype(BF)
    qkv = (dot(w_qkv, normed_1, ((0,), (0,))) + qkv_bias).astype(BF)
    queries, keys, values = qkv.reshape(3, heads, HEAD_DIM, length)
    mixed_heads, log_norms = attend(queries, keys, values)
    mixed = mixed_heads.reshape(split, length)
    attn_out = links.col_sum(dot(w_o, mixed, ((1,), (0,))), "ea")
    middle = stream + (attn_out + ordered(out_bias))
    unit_2, inverse_2 = unit_of(middle)
    normed_2 = (unit_2 * gain_2 + ordered(norm2_shift)).astype(BF)

    def feed(part):
        hidden_pre = dot(w_1[part], normed_2, ((0,), (0,))) + bias_1[part][:, None]
        below, slope = gelu_parts(hidden_pre)
        grad_activ = dot(w_2[part], grad_out, ((0,), (0,)))
        return (hidden_pre * below).astype(BF), (grad_activ * (below + slope)).astype(BF)

    activ, grad_hidden = zip(feed(1), feed(0))
    activ, grad_hidden = activ[::-1], grad_hidden[::-1]

    def block_grad(left, right, name):
        give = dot(left, right[1], ((1,), (1,))).astype(BF)
        keep = dot(left, right[0], ((1,), (1,))).astype(BF)
        return links.reduce_x(add_low(keep, swap(give, "core", f"{name}_c")), name)

    g_2 = block_grad(grad_out, activ, "g2")
    g_1 = block_grad(normed_2, grad_hidden, "g1")
    share = g_2.shape[1]
    ffn_grad = links.row_scatter(jnp.concatenate([g_2, g_1], axis=1), "gf")
    ffn_grad = jnp.stack([ffn_grad[:, :share], ffn_grad[:, share:]])

    ffn_part = dot(w_2[0], activ[0], ((1,), (0,))) + dot(w_2[1], activ[1], ((1,), (0,)))
    out_half = halves(middle, col) + (links.col_scatter(ffn_part, "ef") + ordered(fc2_bias))
    output = links.clip_out(out_half.astype(BF), "fo")

    part_2 = dot(w_1[0], grad_hidden[0], ((1,), (0,))) + dot(w_1[1], grad_hidden[1], ((1,), (0,)))
    grad_normed_2 = links.col_sum(part_2, "eh")
    middle_grad = upstream + norm_back(grad_normed_2, unit_2, inverse_2, gain_2)
    grad_branch = middle_grad.astype(BF)
    out_part = dot(grad_branch, mixed, ((1,), (1,))).astype(BF)
    grad_mixed = dot(w_o, grad_branch, ((0,), (0,))).astype(BF)
    grads = attend_back(
        queries, keys, values, log_norms, grad_mixed.reshape(heads, HEAD_DIM, length)
    )
    grad_qkv = jnp.concatenate([g.reshape(split, length) for g in grads], axis=0).astype(BF)
    part_1 = dot(w_qkv, grad_qkv, ((1,), (0,)))
    grad_normed_1 = links.col_scatter(part_1, "ei")
    qkv_part = dot(normed_1, grad_qkv, ((1,), (1,))).astype(BF)
    low, high = qkv_part[:, : 2 * split], jnp.concatenate([qkv_part[:, 2 * split :], out_part], 1)
    other = swap(jnp.where(core == 0, high, low), "core", "ga_c")
    g_a = add_low(jnp.where(core == 0, low, high), other)
    attn_grad = links.row_scatter(links.reduce_x_fixed(g_a, "ga"), "ga")
    attn_grad = links.spread(attn_grad, "ga")
    fc2_grad, fc1_grad = links.spread(ffn_grad, "gf")

    unit_1_half = halves(unit_1, col)
    features_half = halves(middle_grad, col) + norm_back(
        grad_normed_1, unit_1_half, halves(inverse_1, col), gain_1
    )
    features_grad = links.clip_out(features_half.astype(BF), "go").astype(F32)

    grad_normed_2_half = halves(grad_normed_2, col)
    by_width = jnp.stack(
        [
            jnp.sum(grad_normed_1 * unit_1_half, axis=1),
            jnp.sum(grad_normed_1, axis=1),
            jnp.sum(grad_normed_2_half * halves(unit_2, col), axis=1),
            jnp.sum(grad_normed_2_half, axis=1),
            jnp.sum(halves(grad_branch, col).astype(F32), axis=1),
            jnp.sum(halves(grad_out, col).astype(F32), axis=1),
        ]
    ).reshape(6, count_row, width)
    inverse = [links.order.index(j) for j in range(count_row)]
    by_width = jnp.stack([by_width[:, i] for i in inverse], axis=1)
    by_width = jnp.stack(
        [lax.dynamic_index_in_dim(by_width, row ^ j, 1, keepdims=False) for j in range(count_row)],
        axis=1,
    )
    sums_qkv = jnp.sum(grad_qkv.astype(F32), axis=1)
    sums_1 = links.vector_back(*(jnp.sum(g.astype(F32), axis=1) for g in grad_hidden))
    by_column = jnp.concatenate([sums_qkv[:split], sums_qkv[2 * split :], sums_1])
    zeros = jnp.zeros_like(by_column)
    packed = jnp.concatenate(
        [
            by_width.reshape(-1),
            jnp.where(col == 0, by_column, zeros),
            jnp.where(col == 0, zeros, by_column),
        ]
    )
    for axis in ("core", "col", "row", "x"):
        for mask in doubled(lax.axis_size(axis), True)[0]:
            packed = packed + swap(packed, axis, f"ve_{axis}{mask}", mask)
    size = 6 * count_row * width
    by_width = lax.dynamic_index_in_dim(
        packed[:size].reshape(6, count_row, width), row, 1, keepdims=False
    )
    by_column = lax.dynamic_index_in_dim(packed[size:].reshape(2, -1), col, 0, keepdims=False)
    return (
        output,
        features_grad,
        attn_grad[:, :split],
        attn_grad[:, split : 2 * split],
        attn_grad[:, 2 * split : 3 * split],
        by_column[:split],
        by_column[split : 2 * split],
        attn_grad[:, 3 * split :],
        by_width[4],
        fc1_grad,
        by_column[2 * split :],
        fc2_grad,
        by_width[5],
        by_width[0],
        by_width[1],
        by_width[2],
        by_width[3],
    )


def solution(mesh):
    count_dp, count_row, count_col = mesh.devices.shape
    fine = Mesh(
        mesh.devices.reshape(count_dp // 2, 2, count_row, count_col), ("x", "core", "row", "col")
    )
    clip = P(("x", "core", "col"), "row", None)
    block, column, row, whole = P("row", "col"), P("col"), P("row"), P()
    return jax.shard_map(
        on_device,
        mesh=fine,
        in_specs=(
            clip,
            clip,
            block,
            block,
            block,
            column,
            column,
            block,
            whole,
            block,
            column,
            block,
            whole,
            whole,
            whole,
            whole,
            whole,
        ),
        out_specs=(
            clip,
            clip,
            block,
            block,
            block,
            column,
            column,
            block,
            row,
            block,
            column,
            block,
            row,
            row,
            row,
            row,
            row,
        ),
        check_vma=False,
    )
```
